768 devices in a mesh: az: 16 (over z_lo, x), rad: 48 (over y, z_hi, core).
Axes of the slice: x: 4, y: 8, z: 12 (z_hi: 3, z_lo: 4; z = z_hi * 4 + z_lo), core: 2. Of those that a mesh axis runs over, the one named last changes fastest.
Arguments:
- fields: float32 [5, 2, 384, 2048], P(None, None, 'rad', 'az'), may hold values from -6 to 6
- velocity: float32 [2, 384, 2048], P(None, 'rad', 'az'), may hold values from -0.5 to 0.5
- offsets: int32 [384], P('rad'), may hold values from 0 to 1024, as said below
Outputs:
- fields_out: float32 [5, 2, 384, 2048], P(None, None, 'rad', 'az')
The draws below stay inside these ranges and needn't reach their ends.
Inputs may be any that keep to these rules, and one draw needn't show every extreme that they name: `offsets`: offsets never rise with the radius; the innermost row has 1024 and the outermost 0.
All inputs are finite; a program needn't handle non-finite values.
Results may differ from the reference program's by a relative error of at most 0.00002.
Values sent between devices are 32-bit elements; how exact they have to be, the bound alone decides.
No kernel may reach another device: no remote copies, remote signals or barrier semaphores. Data moves between devices by JAX's collectives and lax.ppermute only.
A program may use at most 32 MiB of HBM per device.

```python
import jax
import jax.numpy as jnp
from jax import lax

NF = 5
ZC = 2
STEPS = 2
NR = 384
NPHI = 2048


def draw_offsets(key, part):
    half_cycle = NPHI // 2
    values = jax.random.randint(key, (NR,), 0, half_cycle + 1)
    values = -jnp.sort(-values)
    values = values.at[0].set(half_cycle).at[NR - 1].set(0)
    return values.astype(jnp.int32)


def levels(own_key, dims, pieces, low, top_value):
    def one(dim, blocks):
        draws = jax.random.uniform(jax.random.fold_in(jax.random.fold_in(own_key, 6), dim), (blocks,), jnp.float32, low / len(pieces), top_value / len(pieces))
        return jnp.repeat(jnp.exp(draws), dims[dim] // blocks).reshape((-1,) + (1,) * (len(dims) - dim - 1))

    level = one(*pieces[0])
    for cut in pieces[1:]:
        level = level * one(*cut)
    return level


def normal_values(rng, extent, deviation, bound, shards=(), held_as=jnp.bfloat16):
    result = deviation * jax.random.normal(rng, extent, jnp.float32)
    if shards:
        result = result * levels(rng, extent, shards, -0.22, 0.18)
    return jnp.clip(result, -bound, bound).astype(held_as)


def setup_inputs(seed: int = 0) -> dict:
    seeds = jax.random.split(jax.random.key(seed), 4)
    return {
        "fields": normal_values(seeds[0], (NF, ZC, NR, NPHI), 1.0, 6.0, ((2, 48), (3, 16)), jnp.float32),
        "velocity": jnp.clip(jax.random.uniform(seeds[1], (2, NR, NPHI), jnp.float32, -0.5, 0.5) * levels(seeds[1], (2, NR, NPHI), ((1, 48), (2, 16)), -0.4, 0.0), -0.5, 0.5),
        "offsets": draw_offsets(jax.random.fold_in(seeds[3], 71), 0),
    }


viscosity = 0.05


def extend(field):
    padded = jnp.pad(field, ((0, 0), (2, 2), (0, 0)))
    return jnp.concatenate([padded[:, :, -2:], padded, padded[:, :, :2]], axis=2)


def stencil(padded, velocity):
    rows = velocity.shape[1]
    cols = velocity.shape[2]
    centre = padded[:, 2:2 + rows, 2:2 + cols]
    r_m2 = padded[:, 0:rows, 2:2 + cols]
    r_m1 = padded[:, 1:1 + rows, 2:2 + cols]
    r_p1 = padded[:, 3:3 + rows, 2:2 + cols]
    r_p2 = padded[:, 4:4 + rows, 2:2 + cols]
    p_m2 = padded[:, 2:2 + rows, 0:cols]
    p_m1 = padded[:, 2:2 + rows, 1:1 + cols]
    p_p1 = padded[:, 2:2 + rows, 3:3 + cols]
    p_p2 = padded[:, 2:2 + rows, 4:4 + cols]
    slope_r = (r_m2 - 8.0 * r_m1 + 8.0 * r_p1 - r_p2) / 12.0
    slope_p = (p_m2 - 8.0 * p_m1 + 8.0 * p_p1 - p_p2) / 12.0
    curve_r = (-r_m2 + 16.0 * r_m1 - 30.0 * centre + 16.0 * r_p1 - r_p2) / 12.0
    curve_p = (-p_m2 + 16.0 * p_m1 - 30.0 * centre + 16.0 * p_p1 - p_p2) / 12.0
    return -velocity[1] * slope_p - velocity[0] * slope_r + viscosity * (curve_r + curve_p)


def reference(fields, velocity, offsets):
    source_col = (jnp.arange(NPHI, dtype=jnp.int32)[None, :] - offsets[:, None]) % NPHI

    def advance(field):
        state = field
        for step_index in range(STEPS):
            section = state + stencil(extend(state), velocity)
            state = 0.5 * (state + section + stencil(extend(section), velocity))
            state = jnp.take_along_axis(state, jnp.broadcast_to(source_col[None], state.shape), axis=2)
        return state

    return lax.map(advance, fields)
```

```python
import jax
import jax.numpy as jnp
from jax import lax
from jax.experimental import pallas as pl
from jax.experimental.pallas import tpu as pltpu
from jax.sharding import PartitionSpec as P

STEPS = 2
VISCOSITY = 0.05
LANES = 128
ROWS = 8


def around(row, lane):
    blocks = row.shape[0]
    behind = pltpu.roll(row, 1, axis=0)
    ahead = pltpu.roll(row, blocks - 1, axis=0)
    m2 = pltpu.roll(jnp.where(lane >= LANES - 2, behind, row), 2, axis=1)
    m1 = pltpu.roll(jnp.where(lane >= LANES - 1, behind, row), 1, axis=1)
    p1 = pltpu.roll(jnp.where(lane < 1, ahead, row), LANES - 1, axis=1)
    p2 = pltpu.roll(jnp.where(lane < 2, ahead, row), LANES - 2, axis=1)
    return m2, m1, p1, p2


def tendency(load, r, v_r, v_p, lane):
    centre = load(r)
    m2, m1, p1, p2 = around(centre, lane)
    r_m2, r_m1, r_p1, r_p2 = load(r - 2), load(r - 1), load(r + 1), load(r + 2)
    near = (m1 + p1) + (r_m1 + r_p1)
    far = (m2 + p2) + (r_m2 + r_p2)
    slope_p = (p1 - m1) * (8.0 / 12.0) - (p2 - m2) * (1.0 / 12.0)
    slope_r = (r_p1 - r_m1) * (8.0 / 12.0) - (r_p2 - r_m2) * (1.0 / 12.0)
    scale = VISCOSITY / 12.0
    curve = near * (16.0 * scale) - far * scale - centre * (60.0 * scale)
    return centre, curve - v_p * slope_p - v_r * slope_r


def steps_kernel(meta, low, own, high, out, state, section, ring):
    blocks = own.shape[0] // (3 * ROWS)
    lane = lax.broadcasted_iota(jnp.int32, (blocks, LANES), 1)
    has_low = meta[2 * ROWS] > 0
    has_high = meta[2 * ROWS + 1] > 0

    def source(r):
        return (low, own, high)[r // ROWS], r % ROWS

    def arrived(r, part):
        ref, local = source(r)
        return ref[pl.ds(part * ROWS + local, blocks, stride=3 * ROWS), :]

    def inside(r, value):
        if r < ROWS:
            return jnp.where(has_low, value, 0.0)
        if r >= 2 * ROWS:
            return jnp.where(has_high, value, 0.0)
        return value

    def shifted(r, value):
        ring[r, :blocks, :] = value
        ring[r, blocks:, :] = value
        offset = meta[r - ROWS // 2]
        hops = offset // LANES
        rest = offset % LANES
        near = ring[r, pl.ds(blocks - hops, blocks), :]
        far = ring[r, pl.ds(blocks - 1 - hops, blocks), :]
        return pltpu.roll(jnp.where(lane < LANES - rest, near, far), rest, axis=1)

    for r in range(3 * ROWS):
        state[r] = arrived(r, 0)
    margin = 0
    for step in range(STEPS):
        for r in range(margin + 2, 3 * ROWS - margin - 2):
            centre, change = tendency(lambda k: state[k], r, arrived(r, 1), arrived(r, 2), lane)
            section[r] = inside(r, centre + change)
        for r in range(margin + 4, 3 * ROWS - margin - 4):
            centre, change = tendency(lambda k: section[k], r, arrived(r, 1), arrived(r, 2), lane)
            value = shifted(r, inside(r, 0.5 * (state[r] + centre + change)))
            if step + 1 < STEPS:
                state[r] = value
            else:
                out[pl.ds(r - ROWS, blocks, stride=ROWS), :] = value
        margin += 4


def shards(fields, velocity, offsets):
    slabs = fields.shape[0] * fields.shape[1]
    blocks = lax.axis_size("az")
    count = lax.axis_size("rad")
    forward = [(i, i + 1) for i in range(count - 1)]
    backward = [(j, i) for i, j in forward]
    offs_low = lax.ppermute(offsets, "rad", forward)
    offs_high = lax.ppermute(offsets, "rad", backward)
    place = lax.axis_index("rad")
    flags = jnp.stack([(place > 0).astype(jnp.int32), (place < count - 1).astype(jnp.int32)])
    meta = jnp.concatenate([offs_low[ROWS // 2 :], offsets, offs_high[: ROWS // 2], flags])

    sent = jnp.pad(fields.reshape(slabs, ROWS, LANES), ((0, blocks - slabs), (0, 0), (0, 0)))
    speeds = jnp.broadcast_to(velocity.reshape(1, 2 * ROWS, LANES), (blocks, 2 * ROWS, LANES))
    sent = jnp.concatenate([sent, speeds], axis=1)
    own = lax.all_to_all(sent, "az", 0, 0, tiled=True)
    low = lax.ppermute(own, "rad", forward)
    high = lax.ppermute(own, "rad", backward)
    flat = (blocks * 3 * ROWS, LANES)
    vmem = pl.BlockSpec(memory_space=pltpu.VMEM)
    done = pl.pallas_call(
        steps_kernel,
        out_shape=jax.ShapeDtypeStruct((blocks * ROWS, LANES), jnp.float32),
        in_specs=[pl.BlockSpec(memory_space=pltpu.SMEM), vmem, vmem, vmem],
        out_specs=vmem,
        scratch_shapes=[
            pltpu.VMEM((3 * ROWS, blocks, LANES), jnp.float32),
            pltpu.VMEM((3 * ROWS, blocks, LANES), jnp.float32),
            pltpu.VMEM((3 * ROWS, 2 * blocks, LANES), jnp.float32),
        ],
        name="disc_steps",
    )(meta, low.reshape(flat), own.reshape(flat), high.reshape(flat))
    back = lax.all_to_all(done.reshape(blocks, ROWS, LANES), "az", 0, 0, tiled=True)
    return back[:slabs].reshape(fields.shape)


def solution(mesh):
    placed = (P(None, None, "rad", "az"), P(None, "rad", "az"), P("rad"))
    return jax.shard_map(
        shards, mesh=mesh, in_specs=placed, out_specs=P(None, None, "rad", "az"), check_vma=False
    )
```

```python
import jax
import jax.numpy as jnp
from jax import lax
from jax.experimental import pallas as pl
from jax.experimental.pallas import tpu as pltpu
from jax.sharding import PartitionSpec as P

STEPS = 2
VISCOSITY = 0.05
LANES = 128
ROWS = 8
MARGIN = 4 * STEPS


def around(row, lane):
    blocks = row.shape[0]
    behind = pltpu.roll(row, 1, axis=0)
    ahead = pltpu.roll(row, blocks - 1, axis=0)
    m2 = pltpu.roll(jnp.where(lane >= LANES - 2, behind, row), 2, axis=1)
    m1 = pltpu.roll(jnp.where(lane >= LANES - 1, behind, row), 1, axis=1)
    p1 = pltpu.roll(jnp.where(lane < 1, ahead, row), LANES - 1, axis=1)
    p2 = pltpu.roll(jnp.where(lane < 2, ahead, row), LANES - 2, axis=1)
    return m2, m1, p1, p2


def tendency(field, r, v_r, v_p, lane):
    centre = field[r]
    m2, m1, p1, p2 = around(centre, lane)
    r_m2, r_m1, r_p1, r_p2 = field[r - 2], field[r - 1], field[r + 1], field[r + 2]
    near = (m1 + p1) + (r_m1 + r_p1)
    far = (m2 + p2) + (r_m2 + r_p2)
    slope_p = (p1 - m1) * (8.0 / 12.0) - (p2 - m2) * (1.0 / 12.0)
    slope_r = (r_p1 - r_m1) * (8.0 / 12.0) - (r_p2 - r_m2) * (1.0 / 12.0)
    scale = VISCOSITY / 12.0
    curve = near * (16.0 * scale) - far * scale - centre * (60.0 * scale)
    return centre, curve - v_p * slope_p - v_r * slope_r


def gather_kernel(offsets, arrived, block):
    blocks = arrived.shape[0] // (3 * ROWS)
    for k in range(3 * ROWS):
        block[pl.ds(k * blocks, blocks), :] = arrived[pl.ds(k, blocks, stride=3 * ROWS), :]
    line = lax.broadcasted_iota(jnp.int32, (ROWS, LANES), 0)
    shifts = jnp.zeros((ROWS, LANES), jnp.int32)
    for k in range(ROWS):
        shifts = jnp.where(line == k, offsets[k], shifts)
    block[pl.ds(3 * ROWS * blocks, ROWS), :] = shifts.astype(jnp.float32)


def steps_kernel(offsets, own, chip, cross, out, state, section, ring, speed, shifts, sem):
    size = own.shape[0]
    blocks = (size - ROWS) // (3 * ROWS)
    lane = lax.broadcasted_iota(jnp.int32, (blocks, LANES), 1)
    place = lax.axis_index("rad")
    upper = place % 2
    theirs = upper * size
    tails = [
        pltpu.make_async_copy(chip.at[pl.ds(size - ROWS, ROWS)], shifts.at[0], sem.at[0]),
        pltpu.make_async_copy(cross.at[pl.ds(theirs + size - ROWS, ROWS)], shifts.at[1], sem.at[1]),
    ]
    for tail in tails:
        tail.start()
    has_low = place > 0
    has_high = place < lax.axis_size("rad") - 1

    def tidy(part, k, value):
        if part == 0:
            return jnp.where(has_low, value, 0.0)
        return jnp.where(has_high, value, 0.0)

    for k in range(3 * ROWS):
        row = pl.ds(k * blocks, blocks)
        from_chip = chip[row, :]
        from_cross = cross[pl.ds(theirs + k * blocks, blocks), :]
        low = jnp.where(upper == 0, from_cross, from_chip)
        high = jnp.where(upper == 0, from_chip, from_cross)
        kind, local = k // ROWS, k % ROWS
        if kind == 0:
            state[local] = tidy(0, k, low)
            state[ROWS + local] = own[row, :]
            state[2 * ROWS + local] = tidy(1, k, high)
        else:
            speed[kind - 1, local] = low
            speed[kind - 1, ROWS + local] = own[row, :]
            speed[kind - 1, 2 * ROWS + local] = high

    def inside(r, value):
        if r < ROWS:
            return tidy(0, r, value)
        if r >= 2 * ROWS:
            return tidy(1, r, value)
        return value

    def shift_of(r):
        local = r % ROWS
        if r // ROWS == 1:
            return offsets[local]
        from_chip = shifts[0, local, 0]
        from_cross = shifts[1, local, 0]
        if r < ROWS:
            return jnp.where(upper == 0, from_cross, from_chip).astype(jnp.int32)
        return jnp.where(upper == 0, from_chip, from_cross).astype(jnp.int32)

    def shifted(r, value):
        ring[r, :blocks, :] = value
        ring[r, blocks:, :] = value
        offset = shift_of(r)
        hops = offset // LANES
        rest = offset % LANES
        near = ring[r, pl.ds(blocks - hops, blocks), :]
        far = ring[r, pl.ds(blocks - 1 - hops, blocks), :]
        return pltpu.roll(jnp.where(lane < LANES - rest, near, far), rest, axis=1)

    margin = 0
    for step in range(STEPS):
        for r in range(margin + 2, 3 * ROWS - margin - 2):
            centre, change = tendency(state, r, speed[0, r], speed[1, r], lane)
            section[r] = inside(r, centre + change)
        if step == 0:
            for tail in tails:
                tail.wait()
        for r in range(margin + 4, 3 * ROWS - margin - 4):
            centre, change = tendency(section, r, speed[0, r], speed[1, r], lane)
            value = shifted(r, inside(r, 0.5 * (state[r] + centre + change)))
            if step + 1 < STEPS:
                state[r] = value
            else:
                out[pl.ds(r - ROWS, blocks, stride=ROWS), :] = value
        margin += 4


def in_vmem(value):
    return pltpu.with_memory_space_constraint(value, pltpu.VMEM)


def shards(fields, velocity, offsets):
    slabs = fields.shape[0] * fields.shape[1]
    blocks = lax.axis_size("az")
    count = lax.axis_size("rad")
    vmem = pl.BlockSpec(memory_space=pltpu.VMEM)
    smem = pl.BlockSpec(memory_space=pltpu.SMEM)

    sent = jnp.pad(fields.reshape(slabs, ROWS, LANES), ((0, blocks - slabs), (0, 0), (0, 0)))
    speeds = jnp.broadcast_to(velocity.reshape(1, 2 * ROWS, LANES), (blocks, 2 * ROWS, LANES))
    sent = jnp.concatenate([sent, speeds], axis=1)
    arrived = lax.all_to_all(sent, "az", 0, 0, tiled=True)
    size = 3 * ROWS * blocks + ROWS
    own = pl.pallas_call(
        gather_kernel,
        out_shape=pltpu.VMEM((size, LANES), jnp.float32),
        in_specs=[smem, vmem],
        out_specs=vmem,
        name="rows",
    )(offsets, in_vmem(arrived.reshape(blocks * 3 * ROWS, LANES)))

    def device(a, r):
        return a * count + r % count

    partner = [(device(a, r), device(a, r ^ 1)) for a in range(slabs) for r in range(count)]
    pairs = [[device(a, r), device(a, r + 1)] for a in range(slabs) for r in range(1, count, 2)]
    pairs += [[device(a, r), device(a, r + 1)] for a in range(slabs, blocks) for r in range(0, count, 2)]
    chip = lax.ppermute(own, ("az", "rad"), partner)
    cross = lax.all_gather(own, ("az", "rad"), axis_index_groups=pairs, tiled=True)

    done = pl.pallas_call(
        steps_kernel,
        out_shape=pltpu.VMEM((blocks * ROWS, LANES), jnp.float32),
        in_specs=[smem, vmem, vmem, vmem],
        out_specs=vmem,
        scratch_shapes=[
            pltpu.VMEM((3 * ROWS, blocks, LANES), jnp.float32),
            pltpu.VMEM((3 * ROWS, blocks, LANES), jnp.float32),
            pltpu.VMEM((3 * ROWS, 2 * blocks, LANES), jnp.float32),
            pltpu.VMEM((2, 3 * ROWS, blocks, LANES), jnp.float32),
            pltpu.SMEM((2, ROWS, LANES), jnp.float32),
            pltpu.SemaphoreType.DMA((2,)),
        ],
        name="disc_steps",
    )(offsets, in_vmem(own), in_vmem(chip), in_vmem(cross))
    back = lax.all_to_all(done.reshape(blocks, ROWS, LANES), "az", 0, 0, tiled=True)
    return back[:slabs].reshape(fields.shape)


def solution(mesh):
    placed = (P(None, None, "rad", "az"), P(None, "rad", "az"), P("rad"))
    return jax.shard_map(
        shards, mesh=mesh, in_specs=placed, out_specs=P(None, None, "rad", "az"), check_vma=False
    )
```

```python
import jax
import jax.numpy as jnp
from jax import lax
from jax.experimental import pallas as pl
from jax.experimental.pallas import tpu as pltpu
from jax.sharding import PartitionSpec as P

STEPS = 2
VISCOSITY = 0.05
LANES = 128
ROWS = 8
HALO = 4
PARTS = 4


def around(row, lane):
    blocks = row.shape[0]
    behind = pltpu.roll(row, 1, axis=0)
    ahead = pltpu.roll(row, blocks - 1, axis=0)
    m2 = pltpu.roll(jnp.where(lane >= LANES - 2, behind, row), 2, axis=1)
    m1 = pltpu.roll(jnp.where(lane >= LANES - 1, behind, row), 1, axis=1)
    p1 = pltpu.roll(jnp.where(lane < 1, ahead, row), LANES - 1, axis=1)
    p2 = pltpu.roll(jnp.where(lane < 2, ahead, row), LANES - 2, axis=1)
    return m2, m1, p1, p2


def tendency(field, r, v_r, v_p, lane):
    centre = field[r]
    m2, m1, p1, p2 = around(centre, lane)
    r_m2, r_m1, r_p1, r_p2 = field[r - 2], field[r - 1], field[r + 1], field[r + 2]
    near = (m1 + p1) + (r_m1 + r_p1)
    far = (m2 + p2) + (r_m2 + r_p2)
    slope_p = (p1 - m1) * (8.0 / 12.0) - (p2 - m2) * (1.0 / 12.0)
    slope_r = (r_p1 - r_m1) * (8.0 / 12.0) - (r_p2 - r_m2) * (1.0 / 12.0)
    scale = VISCOSITY / 12.0
    curve = near * (16.0 * scale) - far * scale - centre * (60.0 * scale)
    return centre, curve - v_p * slope_p - v_r * slope_r


def row_of(arrived, part, r):
    blocks = arrived.shape[0] // (3 * ROWS)
    return arrived[pl.ds(part * ROWS + r, blocks, stride=3 * ROWS), :]


def send_kernel(fields, velocity, offsets, sent, noted):
    slabs = fields.shape[0] // ROWS
    for k in range(sent.shape[0] // (3 * ROWS)):
        at = k * 3 * ROWS
        if k < slabs:
            sent[pl.ds(at, ROWS), :] = fields[pl.ds(k * ROWS, ROWS), :]
        else:
            sent[pl.ds(at, ROWS), :] = jnp.zeros((ROWS, LANES), jnp.float32)
        sent[pl.ds(at + ROWS, 2 * ROWS), :] = velocity[...]
    noted[...] = jnp.zeros((ROWS, LANES), jnp.float32)
    noted[:1, :ROWS] = offsets[...].astype(jnp.float32)


def show_kernel(noted, arrived, to_chip, to_cross):
    blocks = arrived.shape[0] // (3 * ROWS)
    lane = lax.broadcasted_iota(jnp.int32, (blocks, LANES), 1)
    first = lax.axis_index("rad") % 2 == 0
    slab = [row_of(arrived, 0, r) for r in range(ROWS)]
    speed = [[row_of(arrived, 1 + c, r) for r in range(ROWS)] for c in range(2)]

    def put(ref, part, k, value):
        ref[pl.ds((part * HALO + k) * blocks, blocks), :] = value

    for k in range(HALO):
        r = 2 + k
        centre, change = tendency(slab, r, speed[0][r], speed[1][r], lane)
        put(to_chip, 1, k, centre + change)
        put(to_cross, 1, k, centre + change)
        for part, rows in ((0, slab), (2, speed[0]), (3, speed[1])):
            near_low, near_high = rows[k], rows[ROWS - HALO + k]
            put(to_chip, part, k, jnp.where(first, near_high, near_low))
            put(to_cross, part, k, jnp.where(first, near_low, near_high))
    for ref in (to_chip, to_cross):
        ref[pl.ds(PARTS * HALO * blocks, ROWS), :] = noted[...]


def steps_kernel(arrived, shown, chip, cross, out, state, section, ring, speed, shifts, sem):
    size = shown.shape[0]
    blocks = arrived.shape[0] // (3 * ROWS)
    lane = lax.broadcasted_iota(jnp.int32, (blocks, LANES), 1)
    place = lax.axis_index("rad")
    upper = place % 2
    first = upper == 0
    chip_at = (1 - upper) * size if chip.shape[0] > size else 0
    cross_at = upper * size
    tails = [
        pltpu.make_async_copy(ref.at[pl.ds(at + size - ROWS, ROWS)], shifts.at[i], sem.at[i])
        for i, (ref, at) in enumerate(((shown, 0), (chip, chip_at), (cross, cross_at)))
    ]
    for tail in tails:
        tail.start()
    has_low = place > 0
    has_high = place < lax.axis_size("rad") - 1

    def inside(r, value):
        if r < ROWS:
            return jnp.where(has_low, value, 0.0)
        if r >= 2 * ROWS:
            return jnp.where(has_high, value, 0.0)
        return value

    for r in range(ROWS):
        state[ROWS + r] = row_of(arrived, 0, r)
        for c in range(2):
            speed[c, ROWS + r] = row_of(arrived, 1 + c, r)
    for k in range(HALO):
        section[ROWS + 2 + k] = shown[pl.ds((HALO + k) * blocks, blocks), :]
        for part in range(PARTS):
            start = (part * HALO + k) * blocks
            from_chip = chip[pl.ds(chip_at + start, blocks), :]
            from_cross = cross[pl.ds(cross_at + start, blocks), :]
            low = jnp.where(first, from_cross, from_chip)
            high = jnp.where(first, from_chip, from_cross)
            below, above = ROWS - HALO + k, 2 * ROWS + k
            if part == 0:
                state[below] = inside(below, low)
                state[above] = inside(above, high)
            elif part == 1:
                section[2 + k] = inside(2 + k, low)
                section[2 * ROWS + 2 + k] = inside(2 * ROWS + 2 + k, high)
            else:
                speed[part - 2, below] = low
                speed[part - 2, above] = high

    def shift_of(r):
        local = r % ROWS
        if r // ROWS == 1:
            return shifts[0, 0, local].astype(jnp.int32)
        from_chip = shifts[1, 0, local]
        from_cross = shifts[2, 0, local]
        if r < ROWS:
            return jnp.where(first, from_cross, from_chip).astype(jnp.int32)
        return jnp.where(first, from_chip, from_cross).astype(jnp.int32)

    def shifted(r, value):
        ring[r, :blocks, :] = value
        ring[r, blocks:, :] = value
        offset = shift_of(r)
        hops = offset // LANES
        rest = offset % LANES
        near = ring[r, pl.ds(blocks - hops, blocks), :]
        far = ring[r, pl.ds(blocks - 1 - hops, blocks), :]
        return pltpu.roll(jnp.where(lane < LANES - rest, near, far), rest, axis=1)

    margin = 0
    for step in range(STEPS):
        for r in range(margin + 2, 3 * ROWS - margin - 2):
            if step > 0 or not 2 <= r % ROWS < 2 + HALO:
                centre, change = tendency(state, r, speed[0, r], speed[1, r], lane)
                section[r] = inside(r, centre + change)
        if step == 0:
            for tail in tails:
                tail.wait()
        for r in range(margin + 4, 3 * ROWS - margin - 4):
            centre, change = tendency(section, r, speed[0, r], speed[1, r], lane)
            value = shifted(r, inside(r, 0.5 * (state[r] + centre + change)))
            if step + 1 < STEPS:
                state[r] = value
            else:
                out[pl.ds(r - ROWS, blocks, stride=ROWS), :] = value
        margin += 4


def in_vmem(value):
    return pltpu.with_memory_space_constraint(value, pltpu.VMEM)


def shards(fields, velocity, offsets):
    slabs = fields.shape[0] * fields.shape[1]
    blocks = lax.axis_size("az")
    count = lax.axis_size("rad")
    vmem = pl.BlockSpec(memory_space=pltpu.VMEM)

    sent, noted = pl.pallas_call(
        send_kernel,
        out_shape=[
            pltpu.VMEM((blocks * 3 * ROWS, LANES), jnp.float32),
            pltpu.VMEM((ROWS, LANES), jnp.float32),
        ],
        in_specs=[vmem] * 3,
        out_specs=[vmem] * 2,
        name="send",
    )(
        fields.reshape(slabs * ROWS, LANES),
        velocity.reshape(2 * ROWS, LANES),
        offsets.reshape(1, ROWS),
    )
    arrived = lax.all_to_all(sent.reshape(blocks, 3 * ROWS, LANES), "az", 0, 0, tiled=True)
    arrived = in_vmem(arrived.reshape(blocks * 3 * ROWS, LANES))
    size = PARTS * HALO * blocks + ROWS
    to_chip, to_cross = pl.pallas_call(
        show_kernel,
        out_shape=[pltpu.VMEM((size, LANES), jnp.float32)] * 2,
        in_specs=[vmem, vmem],
        out_specs=[vmem, vmem],
        name="show",
    )(in_vmem(noted), arrived)

    def device(a, r):
        return a * count + r % count

    pairs = [[device(a, r), device(a, r + 1)] for a in range(slabs) for r in range(1, count, 2)]
    pairs += [[device(a, r), device(a, r + 1)] for a in range(slabs, blocks) for r in range(0, count, 2)]
    twins = [[r, r + 1] for r in range(0, count, 2)]
    chip = lax.all_gather(to_chip, "rad", axis_index_groups=twins, tiled=True)
    cross = lax.all_gather(to_cross, ("az", "rad"), axis_index_groups=pairs, tiled=True)

    done = pl.pallas_call(
        steps_kernel,
        out_shape=pltpu.VMEM((blocks * ROWS, LANES), jnp.float32),
        in_specs=[vmem] * 4,
        out_specs=vmem,
        scratch_shapes=[
            pltpu.VMEM((3 * ROWS, blocks, LANES), jnp.float32),
            pltpu.VMEM((3 * ROWS, blocks, LANES), jnp.float32),
            pltpu.VMEM((3 * ROWS, 2 * blocks, LANES), jnp.float32),
            pltpu.VMEM((2, 3 * ROWS, blocks, LANES), jnp.float32),
            pltpu.SMEM((3, ROWS, LANES), jnp.float32),
            pltpu.SemaphoreType.DMA((3,)),
        ],
        name="disc_steps",
    )(arrived, in_vmem(to_cross), in_vmem(chip), in_vmem(cross))
    back = lax.all_to_all(done.reshape(blocks, ROWS, LANES), "az", 0, 0, tiled=True)
    return back[:slabs].reshape(fields.shape)


def solution(mesh):
    placed = (P(None, None, "rad", "az"), P(None, "rad", "az"), P("rad"))
    return jax.shard_map(
        shards, mesh=mesh, in_specs=placed, out_specs=P(None, None, "rad", "az"), check_vma=False
    )
```

```python
import jax
import jax.numpy as jnp
from jax import lax
from jax.experimental import pallas as pl
from jax.experimental.pallas import tpu as pltpu
from jax.sharding import PartitionSpec as P

STEPS = 2
VISCOSITY = 0.05
LANES = 128
ROWS = 8
HALO = 4
PARTS = 4


def around(row, lane):
    blocks = row.shape[0]
    behind = pltpu.roll(row, 1, axis=0)
    ahead = pltpu.roll(row, blocks - 1, axis=0)
    m2 = pltpu.roll(jnp.where(lane >= LANES - 2, behind, row), 2, axis=1)
    m1 = pltpu.roll(jnp.where(lane >= LANES - 1, behind, row), 1, axis=1)
    p1 = pltpu.roll(jnp.where(lane < 1, ahead, row), LANES - 1, axis=1)
    p2 = pltpu.roll(jnp.where(lane < 2, ahead, row), LANES - 2, axis=1)
    return m2, m1, p1, p2


def tendency(field, r, v_r, v_p, lane):
    centre = field[r]
    m2, m1, p1, p2 = around(centre, lane)
    r_m2, r_m1, r_p1, r_p2 = field[r - 2], field[r - 1], field[r + 1], field[r + 2]
    near = (m1 + p1) + (r_m1 + r_p1)
    far = (m2 + p2) + (r_m2 + r_p2)
    slope_p = (p1 - m1) * (8.0 / 12.0) - (p2 - m2) * (1.0 / 12.0)
    slope_r = (r_p1 - r_m1) * (8.0 / 12.0) - (r_p2 - r_m2) * (1.0 / 12.0)
    scale = VISCOSITY / 12.0
    curve = near * (16.0 * scale) - far * scale - centre * (60.0 * scale)
    return centre, curve - v_p * slope_p - v_r * slope_r


def row_of(arrived, part, r):
    blocks = arrived.shape[0] // (3 * ROWS)
    return arrived[pl.ds(part * ROWS + r, blocks, stride=3 * ROWS), :]


def send_kernel(fields, velocity, offsets, sent, noted):
    slabs = fields.shape[0] // ROWS
    for k in range(sent.shape[0] // (3 * ROWS)):
        at = k * 3 * ROWS
        if k < slabs:
            sent[pl.ds(at, ROWS), :] = fields[pl.ds(k * ROWS, ROWS), :]
        else:
            sent[pl.ds(at, ROWS), :] = jnp.zeros((ROWS, LANES), jnp.float32)
        sent[pl.ds(at + ROWS, 2 * ROWS), :] = velocity[...]
    noted[...] = jnp.zeros((ROWS, LANES), jnp.float32)
    noted[:1, :ROWS] = offsets[...].astype(jnp.float32)


def show_kernel(noted, arrived, to_chip, to_cross):
    blocks = arrived.shape[0] // (3 * ROWS)
    lane = lax.broadcasted_iota(jnp.int32, (blocks, LANES), 1)
    first = lax.axis_index("rad") % 2 == 0
    slab = [row_of(arrived, 0, r) for r in range(ROWS)]
    speed = [[row_of(arrived, 1 + c, r) for r in range(ROWS)] for c in range(2)]

    def put(ref, part, k, value):
        ref[pl.ds((part * HALO + k) * blocks, blocks), :] = value

    for k in range(HALO):
        r = 2 + k
        centre, change = tendency(slab, r, speed[0][r], speed[1][r], lane)
        put(to_chip, 1, k, centre + change)
        put(to_cross, 1, k, centre + change)
        for part, rows in ((0, slab), (2, speed[0]), (3, speed[1])):
            near_low, near_high = rows[k], rows[ROWS - HALO + k]
            put(to_chip, part, k, jnp.where(first, near_high, near_low))
            put(to_cross, part, k, jnp.where(first, near_low, near_high))
    for ref in (to_chip, to_cross):
        ref[pl.ds(PARTS * HALO * blocks, ROWS), :] = noted[...]


def steps_kernel(arrived, shown, chip, cross, out, state, section, ring, speed, shifts, sem):
    size = shown.shape[0]
    blocks = arrived.shape[0] // (3 * ROWS)
    lane = lax.broadcasted_iota(jnp.int32, (blocks, LANES), 1)
    place = lax.axis_index("rad")
    upper = place % 2
    first = upper == 0
    chip_at = (1 - upper) * size if chip.shape[0] > size else 0
    cross_at = upper * size if cross.shape[0] > size else 0
    tails = [
        pltpu.make_async_copy(ref.at[pl.ds(at + size - ROWS, ROWS)], shifts.at[i], sem.at[i])
        for i, (ref, at) in enumerate(((shown, 0), (chip, chip_at), (cross, cross_at)))
    ]
    for tail in tails:
        tail.start()
    has_low = place > 0
    has_high = place < lax.axis_size("rad") - 1

    def inside(r, value):
        if r < ROWS:
            return jnp.where(has_low, value, 0.0)
        if r >= 2 * ROWS:
            return jnp.where(has_high, value, 0.0)
        return value

    for r in range(ROWS):
        state[ROWS + r] = row_of(arrived, 0, r)
        for c in range(2):
            speed[c, ROWS + r] = row_of(arrived, 1 + c, r)
    for k in range(HALO):
        section[ROWS + 2 + k] = shown[pl.ds((HALO + k) * blocks, blocks), :]
        for part in range(PARTS):
            start = (part * HALO + k) * blocks
            from_chip = chip[pl.ds(chip_at + start, blocks), :]
            from_cross = cross[pl.ds(cross_at + start, blocks), :]
            low = jnp.where(first, from_cross, from_chip)
            high = jnp.where(first, from_chip, from_cross)
            below, above = ROWS - HALO + k, 2 * ROWS + k
            if part == 0:
                state[below] = inside(below, low)
                state[above] = inside(above, high)
            elif part == 1:
                section[2 + k] = inside(2 + k, low)
                section[2 * ROWS + 2 + k] = inside(2 * ROWS + 2 + k, high)
            else:
                speed[part - 2, below] = low
                speed[part - 2, above] = high

    def shift_of(r):
        local = r % ROWS
        if r // ROWS == 1:
            return shifts[0, 0, local].astype(jnp.int32)
        from_chip = shifts[1, 0, local]
        from_cross = shifts[2, 0, local]
        if r < ROWS:
            return jnp.where(first, from_cross, from_chip).astype(jnp.int32)
        return jnp.where(first, from_chip, from_cross).astype(jnp.int32)

    def shifted(r, value):
        ring[r, :blocks, :] = value
        ring[r, blocks:, :] = value
        offset = shift_of(r)
        hops = offset // LANES
        rest = offset % LANES
        near = ring[r, pl.ds(blocks - hops, blocks), :]
        far = ring[r, pl.ds(blocks - 1 - hops, blocks), :]
        return pltpu.roll(jnp.where(lane < LANES - rest, near, far), rest, axis=1)

    margin = 0
    for step in range(STEPS):
        for r in range(margin + 2, 3 * ROWS - margin - 2):
            if step > 0 or not 2 <= r % ROWS < 2 + HALO:
                centre, change = tendency(state, r, speed[0, r], speed[1, r], lane)
                section[r] = inside(r, centre + change)
        if step == 0:
            for tail in tails:
                tail.wait()
        for r in range(margin + 4, 3 * ROWS - margin - 4):
            centre, change = tendency(section, r, speed[0, r], speed[1, r], lane)
            value = shifted(r, inside(r, 0.5 * (state[r] + centre + change)))
            if step + 1 < STEPS:
                state[r] = value
            else:
                out[pl.ds(r - ROWS, blocks, stride=ROWS), :] = value
        margin += 4


def in_vmem(value):
    return pltpu.with_memory_space_constraint(value, pltpu.VMEM)


def shards(fields, velocity, offsets):
    slabs = fields.shape[0] * fields.shape[1]
    blocks = lax.axis_size("az")
    count = lax.axis_size("rad")
    vmem = pl.BlockSpec(memory_space=pltpu.VMEM)

    sent, noted = pl.pallas_call(
        send_kernel,
        out_shape=[
            pltpu.VMEM((blocks * 3 * ROWS, LANES), jnp.float32),
            pltpu.VMEM((ROWS, LANES), jnp.float32),
        ],
        in_specs=[vmem] * 3,
        out_specs=[vmem] * 2,
        name="send",
    )(
        fields.reshape(slabs * ROWS, LANES),
        velocity.reshape(2 * ROWS, LANES),
        offsets.reshape(1, ROWS),
    )
    arrived = lax.all_to_all(sent.reshape(blocks, 3 * ROWS, LANES), "az", 0, 0, tiled=True)
    arrived = in_vmem(arrived.reshape(blocks * 3 * ROWS, LANES))
    size = PARTS * HALO * blocks + ROWS
    to_chip, to_cross = pl.pallas_call(
        show_kernel,
        out_shape=[pltpu.VMEM((size, LANES), jnp.float32)] * 2,
        in_specs=[vmem, vmem],
        out_specs=[vmem, vmem],
        name="show",
    )(in_vmem(noted), arrived)

    def device(a, r):
        return a * count + r % count

    swaps = [(device(a, r), device(a, r + 1)) for a in range(slabs) for r in range(1, count - 1, 2)]
    swaps += [(high, low) for low, high in swaps]
    twins = [[r, r + 1] for r in range(0, count, 2)]
    chip = lax.all_gather(to_chip, "rad", axis_index_groups=twins, tiled=True)
    cross = lax.ppermute(to_cross, ("az", "rad"), swaps)

    done = pl.pallas_call(
        steps_kernel,
        out_shape=pltpu.VMEM((blocks * ROWS, LANES), jnp.float32),
        in_specs=[vmem] * 4,
        out_specs=vmem,
        scratch_shapes=[
            pltpu.VMEM((3 * ROWS, blocks, LANES), jnp.float32),
            pltpu.VMEM((3 * ROWS, blocks, LANES), jnp.float32),
            pltpu.VMEM((3 * ROWS, 2 * blocks, LANES), jnp.float32),
            pltpu.VMEM((2, 3 * ROWS, blocks, LANES), jnp.float32),
            pltpu.SMEM((3, ROWS, LANES), jnp.float32),
            pltpu.SemaphoreType.DMA((3,)),
        ],
        name="disc_steps",
    )(arrived, in_vmem(to_cross), in_vmem(chip), in_vmem(cross))
    back = lax.all_to_all(done.reshape(blocks, ROWS, LANES), "az", 0, 0, tiled=True)
    return back[:slabs].reshape(fields.shape)


def solution(mesh):
    placed = (P(None, None, "rad", "az"), P(None, "rad", "az"), P("rad"))
    return jax.shard_map(
        shards, mesh=mesh, in_specs=placed, out_specs=P(None, None, "rad", "az"), check_vma=False
    )
```

```python
import jax
import jax.numpy as jnp
from jax import lax
from jax.experimental import pallas as pl
from jax.experimental.pallas import tpu as pltpu
from jax.sharding import PartitionSpec as P

STEPS = 2
VISCOSITY = 0.05
LANES = 128
ROWS = 8
HALO = 4
PARTS = 4


def around(row, lane):
    blocks = row.shape[0]
    behind = pltpu.roll(row, 1, axis=0)
    ahead = pltpu.roll(row, blocks - 1, axis=0)
    m2 = pltpu.roll(jnp.where(lane >= LANES - 2, behind, row), 2, axis=1)
    m1 = pltpu.roll(jnp.where(lane >= LANES - 1, behind, row), 1, axis=1)
    p1 = pltpu.roll(jnp.where(lane < 1, ahead, row), LANES - 1, axis=1)
    p2 = pltpu.roll(jnp.where(lane < 2, ahead, row), LANES - 2, axis=1)
    return m2, m1, p1, p2


def tendency(field, r, v_r, v_p, lane):
    centre = field[r]
    m2, m1, p1, p2 = around(centre, lane)
    r_m2, r_m1, r_p1, r_p2 = field[r - 2], field[r - 1], field[r + 1], field[r + 2]
    near = (m1 + p1) + (r_m1 + r_p1)
    far = (m2 + p2) + (r_m2 + r_p2)
    slope_p = (p1 - m1) * 8.0 - (p2 - m2)
    slope_r = (r_p1 - r_m1) * 8.0 - (r_p2 - r_m2)
    curve = (near * 16.0 - far - centre * 60.0) * (VISCOSITY / 12.0)
    return centre, curve - v_p * slope_p - v_r * slope_r


def row_of(arrived, part, r):
    blocks = arrived.shape[0] // (3 * ROWS)
    return arrived[pl.ds(part * ROWS + r, blocks, stride=3 * ROWS), :]


def send_kernel(fields, velocity, offsets, sent, noted):
    slabs = fields.shape[0] // ROWS
    blocks = sent.shape[0] // (3 * ROWS)
    speed = velocity[...] * (1.0 / 12.0)
    for k in range(blocks):
        at = k * 3 * ROWS
        if k < slabs:
            sent[pl.ds(at, ROWS), :] = fields[pl.ds(k * ROWS, ROWS), :]
        else:
            sent[pl.ds(at, ROWS), :] = jnp.zeros((ROWS, LANES), jnp.float32)
        sent[pl.ds(at + ROWS, 2 * ROWS), :] = speed
    noted[...] = jnp.zeros((ROWS, LANES), jnp.float32)
    noted[:1, :ROWS] = offsets[...].astype(jnp.float32)


def show_kernel(noted, arrived, to_chip, to_cross):
    blocks = arrived.shape[0] // (3 * ROWS)
    lane = lax.broadcasted_iota(jnp.int32, (blocks, LANES), 1)
    first = lax.axis_index("rad") % 2 == 0
    slab = [row_of(arrived, 0, r) for r in range(ROWS)]
    speed = [[row_of(arrived, 1 + c, r) for r in range(ROWS)] for c in range(2)]

    def put(ref, part, k, value):
        ref[pl.ds((part * HALO + k) * blocks, blocks), :] = value

    for k in range(HALO):
        r = 2 + k
        centre, change = tendency(slab, r, speed[0][r], speed[1][r], lane)
        put(to_chip, 1, k, centre + change)
        put(to_cross, 1, k, centre + change)
        for part, rows in ((0, slab), (2, speed[0]), (3, speed[1])):
            near_low, near_high = rows[k], rows[ROWS - HALO + k]
            put(to_chip, part, k, jnp.where(first, near_high, near_low))
            put(to_cross, part, k, jnp.where(first, near_low, near_high))
    for ref in (to_chip, to_cross):
        ref[pl.ds(PARTS * HALO * blocks, ROWS), :] = noted[...]


def steps_kernel(arrived, shown, chip, cross, out, state, section, ring, speed, shifts, sem):
    size = shown.shape[0]
    blocks = arrived.shape[0] // (3 * ROWS)
    lane = lax.broadcasted_iota(jnp.int32, (blocks, LANES), 1)
    place = lax.axis_index("rad")
    upper = place % 2
    first = upper == 0
    chip_at = (1 - upper) * size if chip.shape[0] > size else 0
    cross_at = upper * size if cross.shape[0] > size else 0
    tails = [
        pltpu.make_async_copy(ref.at[pl.ds(at + size - ROWS, ROWS)], shifts.at[i], sem.at[i])
        for i, (ref, at) in enumerate(((shown, 0), (chip, chip_at), (cross, cross_at)))
    ]
    for tail in tails:
        tail.start()
    has_low = place > 0
    has_high = place < lax.axis_size("rad") - 1

    def inside(r, value):
        if r < ROWS:
            return jnp.where(has_low, value, 0.0)
        if r >= 2 * ROWS:
            return jnp.where(has_high, value, 0.0)
        return value

    for r in range(ROWS):
        state[ROWS + r] = row_of(arrived, 0, r)
        for c in range(2):
            speed[c, ROWS + r] = row_of(arrived, 1 + c, r)
    for k in range(HALO):
        section[ROWS + 2 + k] = shown[pl.ds((HALO + k) * blocks, blocks), :]
        for part in range(PARTS):
            start = (part * HALO + k) * blocks
            from_chip = chip[pl.ds(chip_at + start, blocks), :]
            from_cross = cross[pl.ds(cross_at + start, blocks), :]
            low = jnp.where(first, from_cross, from_chip)
            high = jnp.where(first, from_chip, from_cross)
            below, above = ROWS - HALO + k, 2 * ROWS + k
            if part == 0:
                state[below] = inside(below, low)
                state[above] = inside(above, high)
            elif part == 1:
                section[2 + k] = inside(2 + k, low)
                section[2 * ROWS + 2 + k] = inside(2 * ROWS + 2 + k, high)
            else:
                speed[part - 2, below] = low
                speed[part - 2, above] = high

    def shift_of(r):
        local = r % ROWS
        if r // ROWS == 1:
            return shifts[0, 0, local].astype(jnp.int32)
        from_chip = shifts[1, 0, local]
        from_cross = shifts[2, 0, local]
        if r < ROWS:
            return jnp.where(first, from_cross, from_chip).astype(jnp.int32)
        return jnp.where(first, from_chip, from_cross).astype(jnp.int32)

    def shifted(r):
        offset = shift_of(r)
        hops = offset // LANES
        rest = offset % LANES
        near = ring[r, pl.ds(blocks - hops, blocks), :]
        far = ring[r, pl.ds(blocks - 1 - hops, blocks), :]
        return pltpu.roll(jnp.where(lane < LANES - rest, near, far), rest, axis=1)

    margin = 0
    for step in range(STEPS):
        for r in range(margin + 2, 3 * ROWS - margin - 2):
            if step > 0 or not 2 <= r % ROWS < 2 + HALO:
                centre, change = tendency(state, r, speed[0, r], speed[1, r], lane)
                section[r] = inside(r, centre + change)
        inner = range(margin + 4, 3 * ROWS - margin - 4)
        for r in inner:
            centre, change = tendency(section, r, speed[0, r], speed[1, r], lane)
            value = inside(r, 0.5 * (state[r] + centre + change))
            ring[r, :blocks, :] = value
            ring[r, blocks:, :] = value
        if step == 0:
            for tail in tails:
                tail.wait()
        for r in inner:
            if step + 1 < STEPS:
                state[r] = shifted(r)
            else:
                out[pl.ds(r - ROWS, blocks, stride=ROWS), :] = shifted(r)
        margin += 4


def in_vmem(value):
    return pltpu.with_memory_space_constraint(value, pltpu.VMEM)


def shards(fields, velocity, offsets):
    slabs = fields.shape[0] * fields.shape[1]
    blocks = lax.axis_size("az")
    count = lax.axis_size("rad")
    vmem = pl.BlockSpec(memory_space=pltpu.VMEM)

    sent, noted = pl.pallas_call(
        send_kernel,
        out_shape=[
            pltpu.VMEM((blocks * 3 * ROWS, LANES), jnp.float32),
            pltpu.VMEM((ROWS, LANES), jnp.float32),
        ],
        in_specs=[vmem] * 3,
        out_specs=[vmem] * 2,
        name="send",
    )(
        fields.reshape(slabs * ROWS, LANES),
        velocity.reshape(2 * ROWS, LANES),
        offsets.reshape(1, ROWS),
    )
    arrived = lax.all_to_all(sent.reshape(blocks, 3 * ROWS, LANES), "az", 0, 0, tiled=True)
    arrived = in_vmem(arrived.reshape(blocks * 3 * ROWS, LANES))
    size = PARTS * HALO * blocks + ROWS
    to_chip, to_cross = pl.pallas_call(
        show_kernel,
        out_shape=[pltpu.VMEM((size, LANES), jnp.float32)] * 2,
        in_specs=[vmem, vmem],
        out_specs=[vmem, vmem],
        name="show",
    )(in_vmem(noted), arrived)

    def device(a, r):
        return a * count + r % count

    swaps = [(device(a, r), device(a, r + 1)) for a in range(slabs) for r in range(1, count - 1, 2)]
    swaps += [(high, low) for low, high in swaps]
    twins = [[r, r + 1] for r in range(0, count, 2)]
    chip = lax.all_gather(to_chip, "rad", axis_index_groups=twins, tiled=True)
    cross = lax.ppermute(to_cross, ("az", "rad"), swaps)

    done = pl.pallas_call(
        steps_kernel,
        out_shape=pltpu.VMEM((blocks * ROWS, LANES), jnp.float32),
        in_specs=[vmem] * 4,
        out_specs=vmem,
        scratch_shapes=[
            pltpu.VMEM((3 * ROWS, blocks, LANES), jnp.float32),
            pltpu.VMEM((3 * ROWS, blocks, LANES), jnp.float32),
            pltpu.VMEM((3 * ROWS, 2 * blocks, LANES), jnp.float32),
            pltpu.VMEM((2, 3 * ROWS, blocks, LANES), jnp.float32),
            pltpu.SMEM((3, ROWS, LANES), jnp.float32),
            pltpu.SemaphoreType.DMA((3,)),
        ],
        name="disc_steps",
    )(arrived, in_vmem(to_cross), in_vmem(chip), in_vmem(cross))
    back = lax.all_to_all(done.reshape(blocks, ROWS, LANES), "az", 0, 0, tiled=True)
    return back[:slabs].reshape(fields.shape)


def solution(mesh):
    placed = (P(None, None, "rad", "az"), P(None, "rad", "az"), P("rad"))
    return jax.shard_map(
        shards, mesh=mesh, in_specs=placed, out_specs=P(None, None, "rad", "az"), check_vma=False
    )
```

```python
import jax
import jax.numpy as jnp
from jax import lax
from jax.experimental import pallas as pl
from jax.experimental.pallas import tpu as pltpu
from jax.sharding import PartitionSpec as P

VISCOSITY = 0.05
SCALE = VISCOSITY / 12.0
LANES = 128
ROWS = 8
SHOWN = (2, 2, 4, 4, 2)


def around(row, lane):
    blocks = row.shape[0]
    behind = pltpu.roll(row, 1, axis=0)
    ahead = pltpu.roll(row, blocks - 1, axis=0)
    m2 = pltpu.roll(jnp.where(lane >= LANES - 2, behind, row), 2, axis=1)
    m1 = pltpu.roll(jnp.where(lane >= LANES - 1, behind, row), 1, axis=1)
    p1 = pltpu.roll(jnp.where(lane < 1, ahead, row), LANES - 1, axis=1)
    p2 = pltpu.roll(jnp.where(lane < 2, ahead, row), LANES - 2, axis=1)
    return m2, m1, p1, p2


def along(centre, v_p, lane):
    m2, m1, p1, p2 = around(centre, lane)
    curve = ((m1 + p1) * 16.0 - (m2 + p2) - centre * 60.0) * SCALE
    return curve - v_p * ((p1 - m1) * 8.0 - (p2 - m2))


def across(field, r, v_r):
    weights = (-SCALE - v_r, 16.0 * SCALE + 8.0 * v_r, 16.0 * SCALE - 8.0 * v_r, v_r - SCALE)
    rows = (r - 2, r - 1, r + 1, r + 2)
    return sum(weight * field[row] for weight, row in zip(weights, rows) if row in field)


def tendency(field, r, v_r, v_p, lane):
    centre = field[r]
    m2, m1, p1, p2 = around(centre, lane)
    r_m2, r_m1, r_p1, r_p2 = field[r - 2], field[r - 1], field[r + 1], field[r + 2]
    near = (m1 + p1) + (r_m1 + r_p1)
    far = (m2 + p2) + (r_m2 + r_p2)
    slope_p = (p1 - m1) * 8.0 - (p2 - m2)
    slope_r = (r_p1 - r_m1) * 8.0 - (r_p2 - r_m2)
    curve = (near * 16.0 - far - centre * 60.0) * SCALE
    return curve - v_p * slope_p - v_r * slope_r


def row_of(arrived, part, r):
    blocks = arrived.shape[0] // (3 * ROWS)
    return arrived[pl.ds(part * ROWS + r, blocks, stride=3 * ROWS), :]


def send_kernel(fields, velocity, offsets, sent, noted):
    slabs = fields.shape[0] // ROWS
    blocks = sent.shape[0] // (3 * ROWS)
    speed = velocity[...] * (1.0 / 12.0)
    for k in range(blocks):
        at = k * 3 * ROWS
        if k < slabs:
            sent[pl.ds(at, ROWS), :] = fields[pl.ds(k * ROWS, ROWS), :]
        else:
            sent[pl.ds(at, ROWS), :] = jnp.zeros((ROWS, LANES), jnp.float32)
        sent[pl.ds(at + ROWS, 2 * ROWS), :] = speed
    noted[...] = jnp.zeros((ROWS, LANES), jnp.float32)
    noted[:1, :ROWS] = offsets[...].astype(jnp.float32)


def show_kernel(noted, arrived, to_chip, to_cross, kept):
    blocks = arrived.shape[0] // (3 * ROWS)
    lane = lax.broadcasted_iota(jnp.int32, (blocks, LANES), 1)
    first = lax.axis_index("rad") % 2 == 0
    slab = {r: row_of(arrived, 0, r) for r in range(ROWS)}
    v_r = {r: row_of(arrived, 1, r) for r in range(ROWS)}
    v_p = {r: row_of(arrived, 2, r) for r in range(ROWS)}

    def change(field, r):
        if 2 <= r < ROWS - 2:
            return tendency(field, r, v_r[r], v_p[r], lane)
        return along(field[r], v_p[r], lane) + across(field, r, v_r[r])

    alone = {r: slab[r] + change(slab, r) for r in range(ROWS)}
    for k in range(ROWS - 4):
        kept[pl.ds(k * blocks, blocks), :] = alone[2 + k]
    moved = {r: 0.5 * (slab[r] + alone[r] + change(alone, r)) for r in range(ROWS)}
    at = 0
    for count, rows in zip(SHOWN, (slab, alone, moved, v_r, v_p)):
        for k in range(count):
            near_low, near_high = rows[k], rows[ROWS - count + k]
            to_chip[pl.ds(at, blocks), :] = jnp.where(first, near_high, near_low)
            to_cross[pl.ds(at, blocks), :] = jnp.where(first, near_low, near_high)
            at += blocks
    for ref in (to_chip, to_cross):
        ref[pl.ds(at, ROWS), :] = noted[...]


def steps_kernel(
    arrived, kept, shown, chip, cross, out, state, section, ring, v_r, v_p, shifts, sem
):
    size = shown.shape[0]
    blocks = arrived.shape[0] // (3 * ROWS)
    lane = lax.broadcasted_iota(jnp.int32, (blocks, LANES), 1)
    place = lax.axis_index("rad")
    first = place % 2 == 0
    chip_at = (1 - place % 2) * size
    tails = [
        pltpu.make_async_copy(ref.at[pl.ds(at + size - ROWS, ROWS)], shifts.at[i], sem.at[i])
        for i, (ref, at) in enumerate(((shown, 0), (chip, chip_at), (cross, 0)))
    ]
    for tail in tails:
        tail.start()
    has_low = place > 0
    has_high = place < lax.axis_size("rad") - 1

    def inside(r, value):
        if r < ROWS:
            return jnp.where(has_low, value, 0.0)
        if r >= 2 * ROWS:
            return jnp.where(has_high, value, 0.0)
        return value

    for r in range(ROWS):
        state[ROWS + r] = row_of(arrived, 0, r)
        v_r[ROWS + r] = row_of(arrived, 1, r)
        v_p[ROWS + r] = row_of(arrived, 2, r)
    for k in range(ROWS - 4):
        section[ROWS + 2 + k] = kept[pl.ds(k * blocks, blocks), :]
    alone, moved = {}, {}
    at = 0
    for count, rows in zip(SHOWN, (state, alone, moved, v_r, v_p)):
        for k in range(count):
            from_chip = chip[pl.ds(chip_at + at, blocks), :]
            from_cross = cross[pl.ds(at, blocks), :]
            low, high = ROWS - count + k, 2 * ROWS + k
            rows[low] = inside(low, jnp.where(first, from_cross, from_chip))
            rows[high] = inside(high, jnp.where(first, from_chip, from_cross))
            at += blocks

    own = {r: state[r] for r in (8, 9, 14, 15)}
    bring = {r: inside(r, across(own, r, v_r[r])) for r in (6, 7, 16, 17)}
    for r in bring:
        section[r] = alone[r] + bring[r]
    for r in (8, 9, 14, 15):
        section[r] = state[r] + tendency(state, r, v_r[r], v_p[r], lane)

    def shift_of(r):
        local = r % ROWS
        if r // ROWS == 1:
            return shifts[0, 0, local].astype(jnp.int32)
        from_chip = shifts[1, 0, local]
        from_cross = shifts[2, 0, local]
        if r < ROWS:
            return jnp.where(first, from_cross, from_chip).astype(jnp.int32)
        return jnp.where(first, from_chip, from_cross).astype(jnp.int32)

    def shifted(r):
        offset = shift_of(r)
        hops = offset // LANES
        rest = offset % LANES
        near = ring[r, pl.ds(blocks - hops, blocks), :]
        far = ring[r, pl.ds(blocks - 1 - hops, blocks), :]
        return pltpu.roll(jnp.where(lane < LANES - rest, near, far), rest, axis=1)

    def renew(r, value):
        ring[r, :blocks, :] = value
        ring[r, blocks:, :] = value

    def heun(r):
        return 0.5 * (state[r] + section[r] + tendency(section, r, v_r[r], v_p[r], lane))

    for r in range(ROWS, 2 * ROWS):
        renew(r, heun(r))
    bring.update({r: section[r] for r in (8, 9, 14, 15)})
    for r in (4, 5, 6, 7, 16, 17, 18, 19):
        gain = across(bring, r, v_r[r])
        if r in bring:
            gain = gain + bring[r] + along(bring[r], v_p[r], lane)
        renew(r, inside(r, moved[r] + 0.5 * gain))
    for tail in tails:
        tail.wait()
    for r in range(4, 20):
        state[r] = shifted(r)
    for r in range(6, 18):
        section[r] = inside(r, state[r] + tendency(state, r, v_r[r], v_p[r], lane))
    for r in range(ROWS, 2 * ROWS):
        renew(r, heun(r))
    for r in range(ROWS, 2 * ROWS):
        out[pl.ds(r - ROWS, blocks, stride=ROWS), :] = shifted(r)


def in_vmem(value):
    return pltpu.with_memory_space_constraint(value, pltpu.VMEM)


def shards(fields, velocity, offsets):
    slabs = fields.shape[0] * fields.shape[1]
    blocks = lax.axis_size("az")
    count = lax.axis_size("rad")
    vmem = pl.BlockSpec(memory_space=pltpu.VMEM)

    sent, noted = pl.pallas_call(
        send_kernel,
        out_shape=[
            pltpu.VMEM((blocks * 3 * ROWS, LANES), jnp.float32),
            pltpu.VMEM((ROWS, LANES), jnp.float32),
        ],
        in_specs=[vmem] * 3,
        out_specs=[vmem] * 2,
        name="send",
    )(
        fields.reshape(slabs * ROWS, LANES),
        velocity.reshape(2 * ROWS, LANES),
        offsets.reshape(1, ROWS),
    )
    arrived = lax.all_to_all(sent.reshape(blocks, 3 * ROWS, LANES), "az", 0, 0, tiled=True)
    arrived = in_vmem(arrived.reshape(blocks * 3 * ROWS, LANES))
    size = sum(SHOWN) * blocks + ROWS
    to_chip, to_cross, kept = pl.pallas_call(
        show_kernel,
        out_shape=[pltpu.VMEM((rows, LANES), jnp.float32) for rows in (size, size, (ROWS - 4) * blocks)],
        in_specs=[vmem] * 2,
        out_specs=[vmem] * 3,
        name="show",
    )(in_vmem(noted), arrived)

    def device(a, r):
        return a * count + r % count

    swaps = [(device(a, r), device(a, r + 1)) for a in range(slabs) for r in range(1, count - 1, 2)]
    swaps += [(high, low) for low, high in swaps]
    twins = [[r, r + 1] for r in range(0, count, 2)]
    chip = lax.all_gather(to_chip, "rad", axis_index_groups=twins, tiled=True)
    cross = lax.ppermute(to_cross, ("az", "rad"), swaps)

    done = pl.pallas_call(
        steps_kernel,
        out_shape=pltpu.VMEM((blocks * ROWS, LANES), jnp.float32),
        in_specs=[vmem] * 5,
        out_specs=vmem,
        scratch_shapes=[
            pltpu.VMEM((3 * ROWS, blocks, LANES), jnp.float32),
            pltpu.VMEM((3 * ROWS, blocks, LANES), jnp.float32),
            pltpu.VMEM((3 * ROWS, 2 * blocks, LANES), jnp.float32),
            pltpu.VMEM((3 * ROWS, blocks, LANES), jnp.float32),
            pltpu.VMEM((3 * ROWS, blocks, LANES), jnp.float32),
            pltpu.SMEM((3, ROWS, LANES), jnp.float32),
            pltpu.SemaphoreType.DMA((3,)),
        ],
        name="disc_steps",
    )(arrived, in_vmem(kept), in_vmem(to_cross), in_vmem(chip), in_vmem(cross))
    back = lax.all_to_all(done.reshape(blocks, ROWS, LANES), "az", 0, 0, tiled=True)
    return back[:slabs].reshape(fields.shape)


def solution(mesh):
    placed = (P(None, None, "rad", "az"), P(None, "rad", "az"), P("rad"))
    return jax.shard_map(
        shards, mesh=mesh, in_specs=placed, out_specs=P(None, None, "rad", "az"), check_vma=False
    )
```

```python
import jax
import jax.numpy as jnp
from jax import lax
from jax.experimental import pallas as pl
from jax.experimental.pallas import tpu as pltpu
from jax.sharding import PartitionSpec as P

VISCOSITY = 0.05
SCALE = VISCOSITY / 12.0
LANES = 128
ROWS = 8
SHOWN = (2, 2, 4, 4, 2)


def around(row, lane):
    blocks = row.shape[0]
    behind = pltpu.roll(row, 1, axis=0)
    ahead = pltpu.roll(row, blocks - 1, axis=0)
    m2 = pltpu.roll(jnp.where(lane >= LANES - 2, behind, row), 2, axis=1)
    m1 = pltpu.roll(jnp.where(lane >= LANES - 1, behind, row), 1, axis=1)
    p1 = pltpu.roll(jnp.where(lane < 1, ahead, row), LANES - 1, axis=1)
    p2 = pltpu.roll(jnp.where(lane < 2, ahead, row), LANES - 2, axis=1)
    return m2, m1, p1, p2


def along(centre, v_p, lane):
    m2, m1, p1, p2 = around(centre, lane)
    curve = ((m1 + p1) * 16.0 - (m2 + p2) - centre * 60.0) * SCALE
    return curve - v_p * ((p1 - m1) * 8.0 - (p2 - m2))


def across(field, r, v_r):
    weights = (-SCALE - v_r, 16.0 * SCALE + 8.0 * v_r, 16.0 * SCALE - 8.0 * v_r, v_r - SCALE)
    rows = (r - 2, r - 1, r + 1, r + 2)
    return sum(weight * field[row] for weight, row in zip(weights, rows) if row in field)


def tendency(field, r, v_r, v_p, lane):
    centre = field[r]
    m2, m1, p1, p2 = around(centre, lane)
    r_m2, r_m1, r_p1, r_p2 = field[r - 2], field[r - 1], field[r + 1], field[r + 2]
    near = (m1 + p1) + (r_m1 + r_p1)
    far = (m2 + p2) + (r_m2 + r_p2)
    slope_p = (p1 - m1) * 8.0 - (p2 - m2)
    slope_r = (r_p1 - r_m1) * 8.0 - (r_p2 - r_m2)
    curve = (near * 16.0 - far - centre * 60.0) * SCALE
    return curve - v_p * slope_p - v_r * slope_r


def row_of(arrived, part, r):
    blocks = arrived.shape[0] // (3 * ROWS)
    return arrived[pl.ds(part * ROWS + r, blocks, stride=3 * ROWS), :]


def send_kernel(fields, velocity, offsets, sent, noted):
    slabs = fields.shape[0] // ROWS
    blocks = sent.shape[0] // (3 * ROWS)
    speed = velocity[...] * (1.0 / 12.0)
    for k in range(blocks):
        at = k * 3 * ROWS
        if k < slabs:
            sent[pl.ds(at, ROWS), :] = fields[pl.ds(k * ROWS, ROWS), :]
        else:
            sent[pl.ds(at, ROWS), :] = jnp.zeros((ROWS, LANES), jnp.float32)
        sent[pl.ds(at + ROWS, 2 * ROWS), :] = speed
    noted[...] = jnp.zeros((ROWS, LANES), jnp.float32)
    noted[:1, :ROWS] = offsets[...].astype(jnp.float32)


def show_kernel(noted, arrived, to_chip, to_cross, kept):
    blocks = arrived.shape[0] // (3 * ROWS)
    lane = lax.broadcasted_iota(jnp.int32, (blocks, LANES), 1)
    first = lax.axis_index("rad") % 2 == 0
    slab = {r: row_of(arrived, 0, r) for r in range(ROWS)}
    v_r = {r: row_of(arrived, 1, r) for r in range(ROWS)}
    v_p = {r: row_of(arrived, 2, r) for r in range(ROWS)}

    def change(field, r):
        if 2 <= r < ROWS - 2:
            return tendency(field, r, v_r[r], v_p[r], lane)
        return along(field[r], v_p[r], lane) + across(field, r, v_r[r])

    alone = {r: slab[r] + change(slab, r) for r in range(ROWS)}
    for k in range(ROWS - 4):
        kept[pl.ds(k * blocks, blocks), :] = alone[2 + k]
    moved = {r: 0.5 * (slab[r] + alone[r] + change(alone, r)) for r in range(ROWS)}
    at = 0
    for count, rows in zip(SHOWN, (slab, alone, moved, v_r, v_p)):
        for k in range(count):
            near_low, near_high = rows[k], rows[ROWS - count + k]
            to_chip[pl.ds(at, blocks), :] = jnp.where(first, near_high, near_low)
            to_cross[pl.ds(at, blocks), :] = jnp.where(first, near_low, near_high)
            at += blocks
    for ref in (to_chip, to_cross):
        ref[pl.ds(at, ROWS), :] = noted[...]


def steps_kernel(arrived, kept, shown, chip, cross, out, state, section, ring, v_r, v_p):
    size = shown.shape[0]
    blocks = arrived.shape[0] // (3 * ROWS)
    lane = lax.broadcasted_iota(jnp.int32, (blocks, LANES), 1)
    place = lax.axis_index("rad")
    first = place % 2 == 0
    chip_at = (1 - place % 2) * size
    has_low = place > 0
    has_high = place < lax.axis_size("rad") - 1

    def inside(r, value):
        if r < ROWS:
            return jnp.where(has_low, value, 0.0)
        if r >= 2 * ROWS:
            return jnp.where(has_high, value, 0.0)
        return value

    for r in range(ROWS):
        state[ROWS + r] = row_of(arrived, 0, r)
        v_r[ROWS + r] = row_of(arrived, 1, r)
        v_p[ROWS + r] = row_of(arrived, 2, r)
    for k in range(ROWS - 4):
        section[ROWS + 2 + k] = kept[pl.ds(k * blocks, blocks), :]
    alone, moved = {}, {}
    at = 0
    for count, rows in zip(SHOWN, (state, alone, moved, v_r, v_p)):
        for k in range(count):
            from_chip = chip[pl.ds(chip_at + at, blocks), :]
            from_cross = cross[pl.ds(at, blocks), :]
            low, high = ROWS - count + k, 2 * ROWS + k
            rows[low] = inside(low, jnp.where(first, from_cross, from_chip))
            rows[high] = inside(high, jnp.where(first, from_chip, from_cross))
            at += blocks

    own = {r: state[r] for r in (8, 9, 14, 15)}
    bring = {r: inside(r, across(own, r, v_r[r])) for r in (6, 7, 16, 17)}
    for r in bring:
        section[r] = alone[r] + bring[r]
    for r in (8, 9, 14, 15):
        section[r] = state[r] + tendency(state, r, v_r[r], v_p[r], lane)

    tail = pl.ds(size - ROWS, 1)
    from_chip, from_cross = chip[pl.ds(chip_at + size - ROWS, 1), :], cross[tail, :]
    noted = (
        jnp.where(first, from_cross, from_chip),
        shown[tail, :],
        jnp.where(first, from_chip, from_cross),
    )
    cell = lax.broadcasted_iota(jnp.int32, (1, LANES), 1)
    offsets = {
        r: jnp.sum(jnp.where(cell == r % ROWS, noted[r // ROWS], 0.0)).astype(jnp.int32)
        for r in range(4, 20)
    }

    def shifted(r):
        hops = offsets[r] // LANES
        rest = offsets[r] % LANES
        near = ring[r, pl.ds(blocks - hops, blocks), :]
        far = ring[r, pl.ds(blocks - 1 - hops, blocks), :]
        return pltpu.roll(jnp.where(lane < LANES - rest, near, far), rest, axis=1)

    def renew(r, value):
        ring[r, :blocks, :] = value
        ring[r, blocks:, :] = value

    def heun(r):
        return 0.5 * (state[r] + section[r] + tendency(section, r, v_r[r], v_p[r], lane))

    for r in range(ROWS, 2 * ROWS):
        renew(r, heun(r))
    bring.update({r: section[r] for r in (8, 9, 14, 15)})
    for r in (4, 5, 6, 7, 16, 17, 18, 19):
        gain = across(bring, r, v_r[r])
        if r in bring:
            gain = gain + bring[r] + along(bring[r], v_p[r], lane)
        renew(r, inside(r, moved[r] + 0.5 * gain))
    for r in range(4, 20):
        state[r] = shifted(r)
    for r in range(6, 18):
        section[r] = inside(r, state[r] + tendency(state, r, v_r[r], v_p[r], lane))
    for r in range(ROWS, 2 * ROWS):
        renew(r, heun(r))
    for r in range(ROWS, 2 * ROWS):
        out[pl.ds(r - ROWS, blocks, stride=ROWS), :] = shifted(r)


def in_vmem(value):
    return pltpu.with_memory_space_constraint(value, pltpu.VMEM)


def shards(fields, velocity, offsets):
    slabs = fields.shape[0] * fields.shape[1]
    blocks = lax.axis_size("az")
    count = lax.axis_size("rad")
    vmem = pl.BlockSpec(memory_space=pltpu.VMEM)

    sent, noted = pl.pallas_call(
        send_kernel,
        out_shape=[
            pltpu.VMEM((blocks * 3 * ROWS, LANES), jnp.float32),
            pltpu.VMEM((ROWS, LANES), jnp.float32),
        ],
        in_specs=[vmem] * 3,
        out_specs=[vmem] * 2,
        name="send",
    )(
        fields.reshape(slabs * ROWS, LANES),
        velocity.reshape(2 * ROWS, LANES),
        offsets.reshape(1, ROWS),
    )
    arrived = lax.all_to_all(sent.reshape(blocks, 3 * ROWS, LANES), "az", 0, 0, tiled=True)
    arrived = in_vmem(arrived.reshape(blocks * 3 * ROWS, LANES))
    size = sum(SHOWN) * blocks + ROWS
    to_chip, to_cross, kept = pl.pallas_call(
        show_kernel,
        out_shape=[pltpu.VMEM((rows, LANES), jnp.float32) for rows in (size, size, (ROWS - 4) * blocks)],
        in_specs=[vmem] * 2,
        out_specs=[vmem] * 3,
        name="show",
    )(in_vmem(noted), arrived)

    def device(a, r):
        return a * count + r % count

    swaps = [(device(a, r), device(a, r + 1)) for a in range(slabs) for r in range(1, count - 1, 2)]
    swaps += [(high, low) for low, high in swaps]
    twins = [[r, r + 1] for r in range(0, count, 2)]
    chip = lax.all_gather(to_chip, "rad", axis_index_groups=twins, tiled=True)
    cross = lax.ppermute(to_cross, ("az", "rad"), swaps)

    done = pl.pallas_call(
        steps_kernel,
        out_shape=pltpu.VMEM((blocks * ROWS, LANES), jnp.float32),
        in_specs=[vmem] * 5,
        out_specs=vmem,
        scratch_shapes=[
            pltpu.VMEM((3 * ROWS, blocks, LANES), jnp.float32),
            pltpu.VMEM((3 * ROWS, blocks, LANES), jnp.float32),
            pltpu.VMEM((3 * ROWS, 2 * blocks, LANES), jnp.float32),
            pltpu.VMEM((3 * ROWS, blocks, LANES), jnp.float32),
            pltpu.VMEM((3 * ROWS, blocks, LANES), jnp.float32),
        ],
        name="disc_steps",
    )(arrived, in_vmem(kept), in_vmem(to_cross), in_vmem(chip), in_vmem(cross))
    back = lax.all_to_all(done.reshape(blocks, ROWS, LANES), "az", 0, 0, tiled=True)
    return back[:slabs].reshape(fields.shape)


def solution(mesh):
    placed = (P(None, None, "rad", "az"), P(None, "rad", "az"), P("rad"))
    return jax.shard_map(
        shards, mesh=mesh, in_specs=placed, out_specs=P(None, None, "rad", "az"), check_vma=False
    )
```

```python
import jax
import jax.numpy as jnp
from jax import lax
from jax.experimental import pallas as pl
from jax.experimental.pallas import tpu as pltpu
from jax.sharding import PartitionSpec as P

VISCOSITY = 0.05
SCALE = VISCOSITY / 12.0
LANES = 128
ROWS = 8
SHOWN = (2, 2, 4, 4, 2)


def around(row, lane):
    blocks = row.shape[0]
    behind = pltpu.roll(row, 1, axis=0)
    ahead = pltpu.roll(row, blocks - 1, axis=0)
    m2 = pltpu.roll(jnp.where(lane >= LANES - 2, behind, row), 2, axis=1)
    m1 = pltpu.roll(jnp.where(lane >= LANES - 1, behind, row), 1, axis=1)
    p1 = pltpu.roll(jnp.where(lane < 1, ahead, row), LANES - 1, axis=1)
    p2 = pltpu.roll(jnp.where(lane < 2, ahead, row), LANES - 2, axis=1)
    return m2, m1, p1, p2


def along(centre, v_p, lane):
    m2, m1, p1, p2 = around(centre, lane)
    curve = ((m1 + p1) * 16.0 - (m2 + p2) - centre * 60.0) * SCALE
    return curve - v_p * ((p1 - m1) * 8.0 - (p2 - m2))


def across(field, r, v_r):
    weights = (-SCALE - v_r, 16.0 * SCALE + 8.0 * v_r, 16.0 * SCALE - 8.0 * v_r, v_r - SCALE)
    rows = (r - 2, r - 1, r + 1, r + 2)
    return sum(weight * field[row] for weight, row in zip(weights, rows) if row in field)


def tendency(field, r, v_r, v_p, lane):
    centre = field[r]
    m2, m1, p1, p2 = around(centre, lane)
    r_m2, r_m1, r_p1, r_p2 = field[r - 2], field[r - 1], field[r + 1], field[r + 2]
    near = (m1 + p1) + (r_m1 + r_p1)
    far = (m2 + p2) + (r_m2 + r_p2)
    slope_p = (p1 - m1) * 8.0 - (p2 - m2)
    slope_r = (r_p1 - r_m1) * 8.0 - (r_p2 - r_m2)
    curve = (near * 16.0 - far - centre * 60.0) * SCALE
    return curve - v_p * slope_p - v_r * slope_r


def row_of(arrived, part, r):
    blocks = arrived.shape[0] // (3 * ROWS)
    return arrived[pl.ds(part * ROWS + r, blocks, stride=3 * ROWS), :]


def send_kernel(fields, velocity, offsets, sent, noted):
    slabs = fields.shape[0] // ROWS
    blocks = sent.shape[0] // (3 * ROWS)
    speed = velocity[...] * (1.0 / 12.0)
    for k in range(blocks):
        at = k * 3 * ROWS
        if k < slabs:
            sent[pl.ds(at, ROWS), :] = fields[pl.ds(k * ROWS, ROWS), :]
        else:
            sent[pl.ds(at, ROWS), :] = jnp.zeros((ROWS, LANES), jnp.float32)
        sent[pl.ds(at + ROWS, 2 * ROWS), :] = speed
    noted[...] = jnp.zeros((ROWS, LANES), jnp.float32)
    noted[:1, :ROWS] = offsets[...].astype(jnp.float32)


def show_kernel(noted, arrived, to_chip, to_cross, kept):
    blocks = arrived.shape[0] // (3 * ROWS)
    lane = lax.broadcasted_iota(jnp.int32, (blocks, LANES), 1)
    first = lax.axis_index("rad") % 2 == 0
    slab = {r: row_of(arrived, 0, r) for r in range(ROWS)}
    v_r = {r: row_of(arrived, 1, r) for r in range(ROWS)}
    v_p = {r: row_of(arrived, 2, r) for r in range(ROWS)}

    def change(field, r):
        if 2 <= r < ROWS - 2:
            return tendency(field, r, v_r[r], v_p[r], lane)
        return along(field[r], v_p[r], lane) + across(field, r, v_r[r])

    alone = {r: slab[r] + change(slab, r) for r in range(ROWS)}
    moved = {r: 0.5 * (slab[r] + alone[r] + change(alone, r)) for r in range(ROWS)}
    for r in range(ROWS):
        kept[pl.ds(r * blocks, blocks), :] = alone[r]
        kept[pl.ds((ROWS + r) * blocks, blocks), :] = moved[r]
    at = 0
    for count, rows in zip(SHOWN, (slab, alone, moved, v_r, v_p)):
        for k in range(count):
            near_low, near_high = rows[k], rows[ROWS - count + k]
            to_chip[pl.ds(at, blocks), :] = jnp.where(first, near_high, near_low)
            to_cross[pl.ds(at, blocks), :] = jnp.where(first, near_low, near_high)
            at += blocks
    for ref in (to_chip, to_cross):
        ref[pl.ds(at, ROWS), :] = noted[...]


def steps_kernel(arrived, kept, shown, chip, cross, out, state, section, ring, v_r, v_p):
    size = shown.shape[0]
    blocks = arrived.shape[0] // (3 * ROWS)
    lane = lax.broadcasted_iota(jnp.int32, (blocks, LANES), 1)
    place = lax.axis_index("rad")
    first = place % 2 == 0
    chip_at = (1 - place % 2) * size
    has_low = place > 0
    has_high = place < lax.axis_size("rad") - 1

    def inside(r, value):
        if r < ROWS:
            return jnp.where(has_low, value, 0.0)
        if r >= 2 * ROWS:
            return jnp.where(has_high, value, 0.0)
        return value

    begun, alone, moved = {}, {}, {}
    for r in range(ROWS):
        begun[ROWS + r] = row_of(arrived, 0, r)
        alone[ROWS + r] = kept[pl.ds(r * blocks, blocks), :]
        moved[ROWS + r] = kept[pl.ds((ROWS + r) * blocks, blocks), :]
        v_r[ROWS + r] = row_of(arrived, 1, r)
        v_p[ROWS + r] = row_of(arrived, 2, r)
    at = 0
    for count, rows in zip(SHOWN, (begun, alone, moved, v_r, v_p)):
        for k in range(count):
            from_chip = chip[pl.ds(chip_at + at, blocks), :]
            from_cross = cross[pl.ds(at, blocks), :]
            low, high = ROWS - count + k, 2 * ROWS + k
            rows[low] = inside(low, jnp.where(first, from_cross, from_chip))
            rows[high] = inside(high, jnp.where(first, from_chip, from_cross))
            at += blocks

    tail = pl.ds(size - ROWS, 1)
    from_chip, from_cross = chip[pl.ds(chip_at + size - ROWS, 1), :], cross[tail, :]
    noted = (
        jnp.where(first, from_cross, from_chip),
        shown[tail, :],
        jnp.where(first, from_chip, from_cross),
    )
    cell = lax.broadcasted_iota(jnp.int32, (1, LANES), 1)
    offsets = {
        r: jnp.sum(jnp.where(cell == r % ROWS, noted[r // ROWS], 0.0)).astype(jnp.int32)
        for r in range(4, 20)
    }

    def shifted(r):
        hops = offsets[r] // LANES
        rest = offsets[r] % LANES
        near = ring[r, pl.ds(blocks - hops, blocks), :]
        far = ring[r, pl.ds(blocks - 1 - hops, blocks), :]
        return pltpu.roll(jnp.where(lane < LANES - rest, near, far), rest, axis=1)

    def renew(r, value):
        ring[r, :blocks, :] = value
        ring[r, blocks:, :] = value

    edge = (6, 7, 8, 9, 14, 15, 16, 17)
    bring = {}
    for r in edge:
        others = {k: begun[k] for k in edge if k // ROWS != r // ROWS}
        bring[r] = inside(r, across(others, r, v_r[r]))
    whole = {r: alone[r] + bring[r] for r in edge}
    for r in range(4, 20):
        gain = across({k: (bring if k // ROWS == r // ROWS else whole)[k] for k in edge}, r, v_r[r])
        if r in bring:
            gain = gain + bring[r] + along(bring[r], v_p[r], lane)
        renew(r, inside(r, moved[r] + 0.5 * gain))
    for r in range(4, 20):
        state[r] = shifted(r)
    for r in range(6, 18):
        section[r] = inside(r, state[r] + tendency(state, r, v_r[r], v_p[r], lane))
    for r in range(ROWS, 2 * ROWS):
        change = tendency(section, r, v_r[r], v_p[r], lane)
        renew(r, 0.5 * (state[r] + section[r] + change))
    for r in range(ROWS, 2 * ROWS):
        out[pl.ds(r - ROWS, blocks, stride=ROWS), :] = shifted(r)


def in_vmem(value):
    return pltpu.with_memory_space_constraint(value, pltpu.VMEM)


def shards(fields, velocity, offsets):
    slabs = fields.shape[0] * fields.shape[1]
    blocks = lax.axis_size("az")
    count = lax.axis_size("rad")
    vmem = pl.BlockSpec(memory_space=pltpu.VMEM)

    sent, noted = pl.pallas_call(
        send_kernel,
        out_shape=[
            pltpu.VMEM((blocks * 3 * ROWS, LANES), jnp.float32),
            pltpu.VMEM((ROWS, LANES), jnp.float32),
        ],
        in_specs=[vmem] * 3,
        out_specs=[vmem] * 2,
        name="send",
    )(
        fields.reshape(slabs * ROWS, LANES),
        velocity.reshape(2 * ROWS, LANES),
        offsets.reshape(1, ROWS),
    )
    arrived = lax.all_to_all(sent.reshape(blocks, 3 * ROWS, LANES), "az", 0, 0, tiled=True)
    arrived = in_vmem(arrived.reshape(blocks * 3 * ROWS, LANES))
    size = sum(SHOWN) * blocks + ROWS
    to_chip, to_cross, kept = pl.pallas_call(
        show_kernel,
        out_shape=[pltpu.VMEM((rows, LANES), jnp.float32) for rows in (size, size, 2 * ROWS * blocks)],
        in_specs=[vmem] * 2,
        out_specs=[vmem] * 3,
        name="show",
    )(in_vmem(noted), arrived)

    def device(a, r):
        return a * count + r % count

    swaps = [(device(a, r), device(a, r + 1)) for a in range(slabs) for r in range(1, count - 1, 2)]
    swaps += [(high, low) for low, high in swaps]
    twins = [[r, r + 1] for r in range(0, count, 2)]
    chip = lax.all_gather(to_chip, "rad", axis_index_groups=twins, tiled=True)
    cross = lax.ppermute(to_cross, ("az", "rad"), swaps)

    done = pl.pallas_call(
        steps_kernel,
        out_shape=pltpu.VMEM((blocks * ROWS, LANES), jnp.float32),
        in_specs=[vmem] * 5,
        out_specs=vmem,
        scratch_shapes=[
            pltpu.VMEM((3 * ROWS, blocks, LANES), jnp.float32),
            pltpu.VMEM((3 * ROWS, blocks, LANES), jnp.float32),
            pltpu.VMEM((3 * ROWS, 2 * blocks, LANES), jnp.float32),
            pltpu.VMEM((3 * ROWS, blocks, LANES), jnp.float32),
            pltpu.VMEM((3 * ROWS, blocks, LANES), jnp.float32),
        ],
        name="disc_steps",
    )(arrived, in_vmem(kept), in_vmem(to_cross), in_vmem(chip), in_vmem(cross))
    back = lax.all_to_all(done.reshape(blocks, ROWS, LANES), "az", 0, 0, tiled=True)
    return back[:slabs].reshape(fields.shape)


def solution(mesh):
    placed = (P(None, None, "rad", "az"), P(None, "rad", "az"), P("rad"))
    return jax.shard_map(
        shards, mesh=mesh, in_specs=placed, out_specs=P(None, None, "rad", "az"), check_vma=False
    )
```

```python
import jax
import jax.numpy as jnp
from jax import lax
from jax.experimental import pallas as pl
from jax.experimental.pallas import tpu as pltpu
from jax.sharding import PartitionSpec as P


VISCOSITY = 0.05
SCALE = VISCOSITY / 12.0
LANES = 128
ROWS = 8
SHOWN = (2, 2, 4, 4, 2)


def around(row, lane):
    blocks = row.shape[0]
    behind = pltpu.roll(row, 1, axis=0)
    ahead = pltpu.roll(row, blocks - 1, axis=0)
    m2 = pltpu.roll(jnp.where(lane >= LANES - 2, behind, row), 2, axis=1)
    m1 = pltpu.roll(jnp.where(lane >= LANES - 1, behind, row), 1, axis=1)
    p1 = pltpu.roll(jnp.where(lane < 1, ahead, row), LANES - 1, axis=1)
    p2 = pltpu.roll(jnp.where(lane < 2, ahead, row), LANES - 2, axis=1)
    return m2, m1, p1, p2


def along(centre, v_p, lane):
    m2, m1, p1, p2 = around(centre, lane)
    curve = ((m1 + p1) * 16.0 - (m2 + p2) - centre * 60.0) * SCALE
    return curve - v_p * ((p1 - m1) * 8.0 - (p2 - m2))


def across(field, r, v_r):
    weights = (-SCALE - v_r, 16.0 * SCALE + 8.0 * v_r, 16.0 * SCALE - 8.0 * v_r, v_r - SCALE)
    rows = (r - 2, r - 1, r + 1, r + 2)
    return sum(weight * field[row] for weight, row in zip(weights, rows) if row in field)


def tendency(field, r, v_r, v_p, lane):
    centre = field[r]
    m2, m1, p1, p2 = around(centre, lane)
    r_m2, r_m1, r_p1, r_p2 = field[r - 2], field[r - 1], field[r + 1], field[r + 2]
    near = (m1 + p1) + (r_m1 + r_p1)
    far = (m2 + p2) + (r_m2 + r_p2)
    slope_p = (p1 - m1) * 8.0 - (p2 - m2)
    slope_r = (r_p1 - r_m1) * 8.0 - (r_p2 - r_m2)
    curve = (near * 16.0 - far - centre * 60.0) * SCALE
    return curve - v_p * slope_p - v_r * slope_r


def row_of(arrived, part, r):
    blocks = arrived.shape[0] // (3 * ROWS)
    return arrived[pl.ds(part * ROWS + r, blocks, stride=3 * ROWS), :]


def send_kernel(fields, velocity, offsets, sent, noted):
    slabs = fields.shape[0] // ROWS
    blocks = sent.shape[0] // (3 * ROWS)
    speed = velocity[...] * (1.0 / 12.0)
    for k in range(blocks):
        at = k * 3 * ROWS
        if k < slabs:
            sent[pl.ds(at, ROWS), :] = fields[pl.ds(k * ROWS, ROWS), :]
        else:
            sent[pl.ds(at, ROWS), :] = jnp.zeros((ROWS, LANES), jnp.float32)
        sent[pl.ds(at + ROWS, 2 * ROWS), :] = speed
    noted[...] = jnp.zeros((ROWS, LANES), jnp.float32)
    noted[:1, :ROWS] = offsets[...].astype(jnp.float32)


def show_kernel(noted, arrived, to_chip, to_cross, kept):
    blocks = arrived.shape[0] // (3 * ROWS)
    lane = lax.broadcasted_iota(jnp.int32, (blocks, LANES), 1)
    first = lax.axis_index("rad") % 2 == 0
    slab = {r: row_of(arrived, 0, r) for r in range(ROWS)}
    v_r = {r: row_of(arrived, 1, r) for r in range(ROWS)}
    v_p = {r: row_of(arrived, 2, r) for r in range(ROWS)}

    def change(field, r):
        if 2 <= r < ROWS - 2:
            return tendency(field, r, v_r[r], v_p[r], lane)
        return along(field[r], v_p[r], lane) + across(field, r, v_r[r])

    alone = {r: slab[r] + change(slab, r) for r in range(ROWS)}
    moved = {r: 0.5 * (slab[r] + alone[r] + change(alone, r)) for r in range(ROWS)}
    for r in range(ROWS):
        kept[pl.ds(r * blocks, blocks), :] = alone[r]
        kept[pl.ds((ROWS + r) * blocks, blocks), :] = moved[r]
    at = 0
    for count, rows in zip(SHOWN, (slab, alone, moved, v_r, v_p)):
        for k in range(count):
            near_low, near_high = rows[k], rows[ROWS - count + k]
            to_chip[pl.ds(at, blocks), :] = jnp.where(first, near_high, near_low)
            to_cross[pl.ds(at, blocks), :] = jnp.where(first, near_low, near_high)
            at += blocks
    for ref in (to_chip, to_cross):
        ref[pl.ds(at, ROWS), :] = noted[...]


def steps_kernel(arrived, kept, shown, chip, cross, out, state, section, ring, v_r, v_p):
    size = shown.shape[0]
    blocks = arrived.shape[0] // (3 * ROWS)
    lane = lax.broadcasted_iota(jnp.int32, (blocks, LANES), 1)
    place = lax.axis_index("rad")
    first = place % 2 == 0
    chip_at = 0
    has_low = place > 0
    has_high = place < lax.axis_size("rad") - 1

    def inside(r, value):
        if r < ROWS:
            return jnp.where(has_low, value, 0.0)
        if r >= 2 * ROWS:
            return jnp.where(has_high, value, 0.0)
        return value

    begun, alone, moved = {}, {}, {}
    for r in range(ROWS):
        begun[ROWS + r] = row_of(arrived, 0, r)
        alone[ROWS + r] = kept[pl.ds(r * blocks, blocks), :]
        moved[ROWS + r] = kept[pl.ds((ROWS + r) * blocks, blocks), :]
        v_r[ROWS + r] = row_of(arrived, 1, r)
        v_p[ROWS + r] = row_of(arrived, 2, r)
    at = 0
    for count, rows in zip(SHOWN, (begun, alone, moved, v_r, v_p)):
        for k in range(count):
            from_chip = chip[pl.ds(chip_at + at, blocks), :]
            from_cross = cross[pl.ds(at, blocks), :]
            low, high = ROWS - count + k, 2 * ROWS + k
            rows[low] = inside(low, jnp.where(first, from_cross, from_chip))
            rows[high] = inside(high, jnp.where(first, from_chip, from_cross))
            at += blocks

    tail = pl.ds(size - ROWS, 1)
    from_chip, from_cross = chip[pl.ds(chip_at + size - ROWS, 1), :], cross[tail, :]
    noted = (
        jnp.where(first, from_cross, from_chip),
        shown[tail, :],
        jnp.where(first, from_chip, from_cross),
    )
    cell = lax.broadcasted_iota(jnp.int32, (1, LANES), 1)
    offsets = {
        r: jnp.sum(jnp.where(cell == r % ROWS, noted[r // ROWS], 0.0)).astype(jnp.int32)
        for r in range(4, 20)
    }

    def shifted(r):
        hops = offsets[r] // LANES
        rest = offsets[r] % LANES
        near = ring[r, pl.ds(blocks - hops, blocks), :]
        far = ring[r, pl.ds(blocks - 1 - hops, blocks), :]
        return pltpu.roll(jnp.where(lane < LANES - rest, near, far), rest, axis=1)

    def renew(r, value):
        ring[r, :blocks, :] = value
        ring[r, blocks:, :] = value

    edge = (6, 7, 8, 9, 14, 15, 16, 17)
    bring = {}
    for r in edge:
        others = {k: begun[k] for k in edge if k // ROWS != r // ROWS}
        bring[r] = inside(r, across(others, r, v_r[r]))
    whole = {r: alone[r] + bring[r] for r in edge}
    for r in range(4, 20):
        gain = across({k: (bring if k // ROWS == r // ROWS else whole)[k] for k in edge}, r, v_r[r])
        if r in bring:
            gain = gain + bring[r] + along(bring[r], v_p[r], lane)
        renew(r, inside(r, moved[r] + 0.5 * gain))
    for r in range(4, 20):
        state[r] = shifted(r)
    for r in range(6, 18):
        section[r] = inside(r, state[r] + tendency(state, r, v_r[r], v_p[r], lane))
    for r in range(ROWS, 2 * ROWS):
        change = tendency(section, r, v_r[r], v_p[r], lane)
        renew(r, 0.5 * (state[r] + section[r] + change))
    for r in range(ROWS, 2 * ROWS):
        out[pl.ds(r - ROWS, blocks, stride=ROWS), :] = shifted(r)


def in_vmem(value):
    return pltpu.with_memory_space_constraint(value, pltpu.VMEM)


def shards(fields, velocity, offsets):
    slabs = fields.shape[0] * fields.shape[1]
    blocks = lax.axis_size("az")
    count = lax.axis_size("rad")
    vmem = pl.BlockSpec(memory_space=pltpu.VMEM)

    sent, noted = pl.pallas_call(
        send_kernel,
        out_shape=[
            pltpu.VMEM((blocks * 3 * ROWS, LANES), jnp.float32),
            pltpu.VMEM((ROWS, LANES), jnp.float32),
        ],
        in_specs=[vmem] * 3,
        out_specs=[vmem] * 2,
        name="send",
    )(
        fields.reshape(slabs * ROWS, LANES),
        velocity.reshape(2 * ROWS, LANES),
        offsets.reshape(1, ROWS),
    )
    arrived = lax.all_to_all(sent.reshape(blocks, 3 * ROWS, LANES), "az", 0, 0, tiled=True)
    arrived = in_vmem(arrived.reshape(blocks * 3 * ROWS, LANES))
    size = sum(SHOWN) * blocks + ROWS
    to_chip, to_cross, kept = pl.pallas_call(
        show_kernel,
        out_shape=[pltpu.VMEM((rows, LANES), jnp.float32) for rows in (size, size, 2 * ROWS * blocks)],
        in_specs=[vmem] * 2,
        out_specs=[vmem] * 3,
        name="show",
    )(in_vmem(noted), arrived)

    def device(a, r):
        return a * count + r % count

    swaps = [(device(a, r), device(a, r + 1)) for a in range(slabs) for r in range(1, count - 1, 2)]
    swaps += [(high, low) for low, high in swaps]
    twins = [(device(a, r), device(a, r ^ 1)) for a in range(slabs) for r in range(count)]
    cross = lax.ppermute(to_cross, ("az", "rad"), swaps)
    chip = lax.ppermute(to_chip, ("az", "rad"), twins)

    done = pl.pallas_call(
        steps_kernel,
        out_shape=pltpu.VMEM((blocks * ROWS, LANES), jnp.float32),
        in_specs=[vmem] * 5,
        out_specs=vmem,
        scratch_shapes=[
            pltpu.VMEM((3 * ROWS, blocks, LANES), jnp.float32),
            pltpu.VMEM((3 * ROWS, blocks, LANES), jnp.float32),
            pltpu.VMEM((3 * ROWS, 2 * blocks, LANES), jnp.float32),
            pltpu.VMEM((3 * ROWS, blocks, LANES), jnp.float32),
            pltpu.VMEM((3 * ROWS, blocks, LANES), jnp.float32),
        ],
        name="disc_steps",
    )(arrived, in_vmem(kept), in_vmem(to_cross), in_vmem(chip), in_vmem(cross))
    back = lax.all_to_all(done.reshape(blocks, ROWS, LANES), "az", 0, 0, tiled=True)
    return back[:slabs].reshape(fields.shape)


def solution(mesh):
    placed = (P(None, None, "rad", "az"), P(None, "rad", "az"), P("rad"))
    return jax.shard_map(
        shards, mesh=mesh, in_specs=placed, out_specs=P(None, None, "rad", "az"), check_vma=False
    )
```
